32 devices in a mesh: ex: 8 (over z, y), tp: 4 (over x, core).
Axes of the slice: x: 2, y: 2, z: 4, core: 2. Of those that a mesh axis runs over, the one named last changes fastest.
Arguments:
- residual_in: bfloat16 [1536, 2880], P('ex', 'tp'), may hold values from -40 to 40
- queries: bfloat16 [1536, 2048], P('ex', 'tp'), may hold values from -4 to 4
- keys_values: bfloat16 [1536, 4, 128], P('ex', 'tp'), may hold values from -4 to 4
- sink_logits: float32 [32], P('tp'), may hold values from 1 to 6
- out_proj: bfloat16 [2048, 2880], P('tp'), may hold values from -0.75 to 0.75
- norm_gain: float32 [2880], replicated, may hold values from 0.25 to 1.75
- routes: int32 [1536, 4], P('ex'), may hold values from 0 to 7, all different within a row; in each aligned block of 192 rows (0 to 191, 192 to 383, ...) at most 160 rows name the same one
- route_scores: int32 [1536, 4], P('ex'), may hold values from 1 to 8
- tenants: int32 [1536], P('ex'), may hold values from 0 to 7
- gate_up: bfloat16 [8, 2880, 2, 1536], P('ex', None, None, 'tp'), may hold values from -0.109375 to 0.109375
- adapter_in: bfloat16 [8, 2880, 128], P('ex'), may hold values from -0.109375 to 0.109375
- adapter_out: bfloat16 [8, 128, 2, 1536], P('ex', None, None, 'tp'), may hold values from -1.5 to 1.5
- down_proj: bfloat16 [8, 1536, 2880], P('ex', 'tp'), may hold values from -0.15625 to 0.15625
Outputs:
- residual_out: bfloat16 [1536, 2880], P('ex', 'tp')
- expert_mix: bfloat16 [1536, 2880], P('ex', 'tp')
The draws below stay inside these ranges and needn't reach their ends.
Inputs may be any that keep to these rules, and one draw needn't show every extreme that they name: `routes`: among the 192 rows of one device (aligned blocks), no expert is named by more than 160 rows, and in every draw some expert is named by exactly 160 rows of some block.
All inputs are finite; a program needn't handle non-finite values.
Results may differ from the reference program's by a relative error of at most 0.023.
Values may be sent and summed in bfloat16 or wider, within the bound.
A program may use at most 128 MiB of HBM per device.

```python
import math
import jax
import jax.numpy as jnp
import numpy as np
from jax import lax

D = 2880
HD = 64
QH = 32
KVH = 4
WINDOW = 128
EXPERTS = 8
TOP = 4
FFE = 1536
TENANTS = 8
RANK = 16
TOK_DEV = 192
TOKENS = 1536
CAP = 160
N_EX = 8
N_TP = 4


def draw_residual_in(key, part):
    key_row, key_col, key_base = jax.random.split(key, 3)
    row_power = jax.random.uniform(key_row, (TOKENS, 1), jnp.float32)
    col_place = jnp.arange(D, dtype=jnp.float32)[None, :] / D
    col_power = 0.5 * col_place + 0.5 * jax.random.uniform(key_col, (1, D), jnp.float32)
    scales = 10.0 ** (row_power + col_power - 1.0)
    base = jnp.clip(jax.random.normal(key_base, (TOKENS, D), jnp.float32), -4.0, 4.0)
    return (base * scales).astype(jnp.bfloat16)


def set_ends(drawn, rng, least, high):
    longest = drawn.shape.index(max(drawn.shape))
    spots = []
    for shift in (0, 1):
        where = [jax.random.randint(jax.random.fold_in(rng, axis), (), 0, length) for axis, length in enumerate(drawn.shape)]
        where[longest] = (where[longest] + shift) % drawn.shape[longest]
        spots.append(tuple(where))
    return drawn.at[spots[0]].set(least).at[spots[1]].set(high)


def block_levels(own_key, extent, cuts, smallest, top_value):
    factor_of = 1.0
    for position, shards_of in cuts:
        steps = jax.random.uniform(jax.random.fold_in(jax.random.fold_in(own_key, 6), position), (shards_of,), jnp.float32, smallest / len(cuts), top_value / len(cuts))
        factor_of = factor_of * jnp.repeat(jnp.exp(steps), extent[position] // shards_of).reshape((-1,) + (1,) * (len(extent) - 1 - position))
    return factor_of


def assign_block(rng, own, number, rows, amount, top, most, lean):
    order = jax.random.permutation(rng, amount)
    heavy_load, ordinary = portions_of(amount, rows * top, most, lean, True), portions_of(amount, rows * top, most, lean, False)
    places = jnp.arange(amount)

    def named(sizes, turn):
        used = int((sizes > 0).sum())
        fixed = max(1, used // 4)
        moved = fixed + (places - fixed + turn * (used - fixed)) % max(1, amount - fixed)
        return jnp.zeros((amount,), jnp.int32).at[order[jnp.where(places < fixed, places, moved)]].set(jnp.asarray(sizes, jnp.int32))

    sizes = jnp.where(number % 4 == 0, named(heavy_load, number // 4), named(ordinary, number - number // 4 - 1))
    mixed = jax.random.permutation(jax.random.fold_in(own, 3), amount)
    source_of, taker = mixed[0:amount // 2 * 2:2], mixed[1:amount // 2 * 2:2]
    room = jnp.minimum(sizes[source_of] - 1, most - sizes[taker]) // 2
    room = jnp.where((source_of == order[0]) | (taker == order[0]) | (sizes[taker] == 0), 0, jnp.maximum(room, 0))
    moved = jax.random.randint(jax.random.fold_in(own, 4), (amount // 2,), 0, 1 << 20) % (room + 1)
    sizes = sizes.at[source_of].add(-moved).at[taker].add(moved)
    labels = jnp.searchsorted(jnp.cumsum(sizes), jnp.arange(rows * top), side="right").astype(jnp.int32)
    table = labels.reshape(top, rows).T
    table = table[jax.random.permutation(jax.random.fold_in(own, 1), rows)]
    turn = jax.random.randint(jax.random.fold_in(own, 2), (rows, 1), 0, top)
    return jnp.take_along_axis(table, (jnp.arange(top)[None, :] + turn) % top, axis=1)


def portions_of(count, total, bound, skew, full):
    weights = [(1 << 20) // math.isqrt(grade ** skew) + 1 for grade in range(1, count + 1)]
    largest = bound if full else min(bound, max(-(-total // count), total * weights[0] // sum(weights)))
    least = 1 if total - largest >= count - 1 else 0
    holding, rest = [largest] + [least] * (count - 1), total - largest - least * (count - 1)
    while rest > 0:
        candidates = [i for i in range(1, count) if holding[i] < largest] or [i for i in range(1, count) if holding[i] < bound]
        whole, remaining = sum([weights[i] for i in candidates]), rest
        for i in candidates:
            addition = min(bound - holding[i], max(1, remaining * weights[i] // whole), rest)
            holding[i] = holding[i] + addition
            rest = rest - addition
    return np.array(holding)


def noise(stream_key, dims, deviation, most, cuts=(), kind=jnp.bfloat16):
    entries = jax.random.normal(stream_key, dims, jnp.float32) * deviation
    if len(cuts) > 0:
        entries = block_levels(stream_key, dims, cuts, -0.22, 0.18) * entries
    return jnp.clip(entries, min=-most, max=most).astype(kind)


def setup_inputs(seed: int = 0) -> dict:
    splits = jax.random.split(jax.random.key(seed), 14)
    residual_in = draw_residual_in(jax.random.fold_in(splits[13], 71), 0)
    queries = noise(splits[1], (TOKENS, QH * HD), 1.0, 4.0, ((0, 8), (1, 4)))
    keys_values = noise(splits[2], (TOKENS, KVH, 2 * HD), 1.0, 4.0, ((0, 8), (1, 4)))
    sink_logits = jnp.clip(1.0 + 5.0 * jax.random.uniform(splits[3], (QH,), jnp.float32) ** block_levels(splits[3], (QH,), ((0, 4),), -0.2, 0.2), 1.0, 6.0)
    out_proj = noise(splits[4], (QH * HD, D), HD ** -0.5, 0.75, ((0, 4),))
    norm_gain = jnp.clip(1.0 + 0.15 * jax.random.normal(splits[5], (D,), jnp.float32), 0.25, 1.75)
    routes_keys = jax.random.split(jax.random.fold_in(splits[6], 1), TOKENS // TOK_DEV)
    routes_turns = jax.random.permutation(jax.random.fold_in(splits[6], 3), TOKENS // TOK_DEV)
    routes = jax.vmap(lambda own, number: assign_block(jax.random.fold_in(splits[6], 2), own, number, TOK_DEV, EXPERTS, TOP, CAP, 2))(routes_keys, routes_turns).reshape((TOKENS, TOP))
    route_scores = set_ends(jax.random.randint(splits[7], (TOKENS, TOP), 1, 9), jax.random.fold_in(splits[7], 1), 1, 8).astype(jnp.int32)
    tenants = set_ends(jax.random.randint(splits[8], (TOKENS,), 0, TENANTS), jax.random.fold_in(splits[8], 1), 0, TENANTS - 1).astype(jnp.int32)
    gate_up = noise(splits[9], (EXPERTS, D, 2, FFE), D ** -0.5, 0.109375, ((0, 8), (3, 4)))
    adapter_in = noise(splits[10], (EXPERTS, D, TENANTS * RANK), D ** -0.5, 0.109375, ((0, 8),))
    adapter_out = noise(splits[11], (EXPERTS, TENANTS * RANK, 2, FFE), RANK ** -0.5, 1.5, ((0, 8), (3, 4)))
    down_proj = noise(splits[12], (EXPERTS, FFE, D), FFE ** -0.5, 0.15625, ((0, 8), (1, 4)))
    return dict(residual_in=residual_in, queries=queries, keys_values=keys_values, sink_logits=sink_logits, out_proj=out_proj, norm_gain=norm_gain, routes=routes, route_scores=route_scores, tenants=tenants, gate_up=gate_up, adapter_in=adapter_in, adapter_out=adapter_out, down_proj=down_proj)


def attend_block(block_id, queries, padded_kv, sink_logits):
    start = block_id * TOK_DEV
    query_rows = lax.dynamic_slice_in_dim(queries, start, TOK_DEV, 0).astype(jnp.float32)
    query_rows = query_rows.reshape(TOK_DEV, KVH, QH // KVH, HD)
    key_rows = lax.dynamic_slice_in_dim(padded_kv, start, TOK_DEV + WINDOW - 1, 0).astype(jnp.float32)
    keys_only = key_rows[:, :, :HD]
    values_only = key_rows[:, :, HD:]
    scores = jnp.einsum('tcgd,jcd->cgtj', query_rows, keys_only) * HD ** (-0.5)
    query_pos = start + jnp.arange(TOK_DEV, dtype=jnp.int32)
    key_pos = start - (WINDOW - 1) + jnp.arange(TOK_DEV + WINDOW - 1, dtype=jnp.int32)
    distance = query_pos[:, None] - key_pos[None, :]
    allowed = (distance >= 0) & (distance < WINDOW) & (key_pos[None, :] >= 0)
    numerators = jnp.where(allowed, jnp.exp(scores), 0.0)
    totals = jnp.exp(sink_logits.reshape(KVH, QH // KVH))[:, :, None] + lax.optimization_barrier(jnp.sum(numerators, axis=-1))
    weights = (numerators / totals[..., None]).astype(jnp.bfloat16)
    result = jnp.einsum('cgtj,jcd->tcgd', weights.astype(jnp.float32), values_only)
    return result.astype(jnp.bfloat16).reshape(TOK_DEV, QH * HD)

def reference(residual_in, queries, keys_values, sink_logits, out_proj, norm_gain, routes, route_scores, tenants, gate_up, adapter_in, adapter_out, down_proj):
    padded_kv = jnp.concatenate([jnp.zeros((WINDOW - 1, KVH, 2 * HD), keys_values.dtype), keys_values], axis=0)
    block_ids = jnp.arange(N_EX, dtype=jnp.int32)
    attended = lax.map(lambda block_id: attend_block(block_id, queries, padded_kv, sink_logits), block_ids)
    attended = attended.reshape(TOKENS, QH * HD)
    projected_heads = jnp.dot(attended, out_proj, preferred_element_type=jnp.float32)
    residual_out = (residual_in.astype(jnp.float32) + projected_heads).astype(jnp.bfloat16)
    widened = lax.optimization_barrier(residual_out).astype(jnp.float32)
    inverse = lax.rsqrt(lax.optimization_barrier(jnp.mean(widened * widened, axis=-1, keepdims=True)) + 1e-05)
    normed = (widened * inverse * norm_gain).astype(jnp.bfloat16)
    pair_count = TOKENS * TOP
    block_routes = routes.reshape(N_EX, TOK_DEV * TOP)
    one_hot = (block_routes[:, :, None] == jnp.arange(EXPERTS, dtype=jnp.int32)[None, None, :]).astype(jnp.int32)
    earlier = jnp.cumsum(one_hot, axis=1) - one_hot
    slot = lax.optimization_barrier(jnp.sum(earlier * one_hot, axis=2))
    source = jnp.arange(N_EX, dtype=jnp.int32)[:, None]
    target = (block_routes * (N_EX * CAP) + source * CAP + slot).reshape(pair_count)
    pair_of = jnp.full((EXPERTS * N_EX * CAP,), pair_count, jnp.int32).at[target].set(jnp.arange(pair_count, dtype=jnp.int32))
    token_of = pair_of // TOP
    score_float = route_scores.astype(jnp.float32)
    route_weight = (score_float / lax.optimization_barrier(jnp.sum(score_float, axis=1, keepdims=True))).reshape(pair_count)
    weight_pad = jnp.concatenate([route_weight, jnp.zeros((1,), jnp.float32)])
    normed_pad = jnp.concatenate([normed, jnp.zeros((1, D), jnp.bfloat16)], axis=0)
    tenant_pad = jnp.concatenate([tenants, jnp.zeros((1,), jnp.int32)])
    slot_tokens = token_of.reshape(EXPERTS, N_EX * CAP)
    slot_weights = weight_pad[pair_of].reshape(EXPERTS, N_EX * CAP)

    def one_expert(carry, packed):
        weight_gu, weight_in, weight_out, weight_down, row_tokens, row_weights = packed
        rows = normed_pad[row_tokens]
        row_tenants = tenant_pad[row_tokens]
        mapped = jnp.dot(rows, weight_gu.reshape(D, 2 * FFE), preferred_element_type=jnp.float32)
        low_rank = jnp.dot(rows, weight_in, preferred_element_type=jnp.float32)
        keep = (jnp.arange(TENANTS * RANK, dtype=jnp.int32) // RANK)[None, :] == row_tenants[:, None]
        low_rank = jnp.where(keep, low_rank, 0.0).astype(jnp.bfloat16)
        mapped = mapped + jnp.dot(low_rank, weight_out.reshape(TENANTS * RANK, 2 * FFE), preferred_element_type=jnp.float32)
        gate_part = mapped[:, :FFE]
        up_part = mapped[:, FFE:]
        activated = (gate_part * jax.nn.sigmoid(1.702 * gate_part) * (up_part + 1.0)).astype(jnp.bfloat16)
        quarters = jnp.einsum('rpf,pfd->prd', activated.astype(jnp.float32).reshape(-1, N_TP, FFE // N_TP), weight_down.astype(jnp.float32).reshape(N_TP, FFE // N_TP, D))
        quarters = lax.optimization_barrier(quarters.astype(jnp.bfloat16)).astype(jnp.float32)
        expert_out = lax.optimization_barrier(jnp.sum(quarters, axis=0))
        return (carry.at[row_tokens].add(expert_out * row_weights[:, None]), None)
    start_mix = jnp.zeros((TOKENS + 1, D), jnp.float32)
    mixed, unused = lax.scan(one_expert, start_mix, (gate_up, adapter_in, adapter_out, down_proj, slot_tokens, slot_weights))
    return (residual_out, mixed[:TOKENS].astype(jnp.bfloat16))
```

```python
import jax
import jax.numpy as jnp
from jax import lax
from jax.sharding import PartitionSpec as P

WINDOW = 128
TOP = 4
RANK = 16


def from_behind(value, axis, steps):
    count = lax.axis_size(axis)
    initial, last = (max(0, -steps), min(count, count - steps))
    return lax.ppermute(value, axis, [(source, source + steps) for source in range(initial, last)])


def shards(
    residual_in,
    queries,
    keys_values,
    sink_logits,
    out_proj,
    norm_gain,
    routes,
    route_scores,
    tenants,
    gate_up,
    adapter_in,
    adapter_out,
    down_proj,
):
    tok_rows = residual_in.shape[0]
    columns = residual_in.shape[1]
    width = out_proj.shape[1]
    heads_here = sink_logits.shape[0]
    kv_here = keys_values.shape[1]
    group_size = heads_here // kv_here
    head_size = keys_values.shape[2] // 2
    rim_rows = WINDOW - 1
    table = token_table(routes, route_scores, tenants, gate_up.shape[0] * lax.axis_size("ex"))
    before = from_behind(keys_values[tok_rows - rim_rows :], "ex", 1)
    extended = jnp.concatenate([before, keys_values], axis=0)
    keys_only = extended[:, :, :head_size]
    values_only = extended[:, :, head_size:]
    query_rows = queries.reshape(tok_rows, kv_here, group_size, head_size)
    scores = jnp.einsum(
        "tcgd,jcd->cgtj", query_rows, keys_only, preferred_element_type=jnp.float32
    ) * head_size ** (-0.5)
    start = lax.axis_index("ex") * tok_rows
    query_pos = start + jnp.arange(tok_rows, dtype=jnp.int32)
    key_pos = start - rim_rows + jnp.arange(tok_rows + rim_rows, dtype=jnp.int32)
    distance = query_pos[:, None] - key_pos[None, :]
    allowed = (distance >= 0) & (distance < WINDOW) & (key_pos[None, :] >= 0)
    numerators = jnp.where(allowed, jnp.exp(scores), 0.0)
    totals = jnp.exp(sink_logits.reshape(kv_here, group_size))[:, :, None] + jnp.sum(
        numerators, axis=-1
    )
    weights = (numerators / totals[..., None]).astype(jnp.bfloat16)
    attended = jnp.einsum(
        "cgtj,jcd->tcgd", weights, values_only, preferred_element_type=jnp.float32
    )
    attended = attended.astype(jnp.bfloat16).reshape(tok_rows, heads_here * head_size)
    head_terms = jnp.dot(attended, out_proj, preferred_element_type=jnp.float32)
    head_share = lax.psum_scatter(
        head_terms.astype(jnp.bfloat16), "tp", scatter_dimension=1, tiled=True
    ).astype(jnp.float32)
    residual_out = (residual_in.astype(jnp.float32) + head_share).astype(jnp.bfloat16)
    sources = lax.axis_size("ex")
    experts_all = gate_up.shape[0] * sources
    capacity = 5 * tok_rows * TOP // (3 * experts_all)
    if gate_up.shape[0] == 1 and 2 * capacity >= tok_rows:
        mixed = dense_experts(
            residual_out, table, norm_gain, gate_up, adapter_in, adapter_out, down_proj
        )
        return (residual_out, mixed)
    return (
        residual_out,
        routed_experts(
            residual_out, norm_gain, routes, route_scores, tenants,
            gate_up, adapter_in, adapter_out, down_proj, columns,
        ),
    )


def token_table(routes, route_scores, tenants, experts_all):
    score_float = route_scores.astype(jnp.float32)
    share = score_float / jnp.sum(score_float, axis=1, keepdims=True)
    hit = routes[:, :, None] == jnp.arange(experts_all, dtype=jnp.int32)[None, None, :]
    by_expert = jnp.sum(jnp.where(hit, share[:, :, None], 0.0), axis=1)
    return jnp.concatenate([by_expert, tenants.astype(jnp.float32)[:, None]], axis=1)


def dense_experts(
    residual_out, table, norm_gain, gate_up, adapter_in, adapter_out, down_proj
):
    tok_rows, columns = residual_out.shape
    sources = lax.axis_size("ex")
    quarters = lax.axis_size("tp")
    width = columns * quarters
    rows_all = sources * tok_rows
    hidden_here = gate_up.shape[3]
    rank_cols = adapter_in.shape[2]
    tokens = gather_tokens(residual_out)
    whole_rows = tokens.astype(jnp.float32)
    inverse = lax.rsqrt(jnp.mean(whole_rows * whole_rows, axis=-1, keepdims=True) + 1e-05)
    normed = (whole_rows * inverse * norm_gain).astype(jnp.bfloat16)
    everyone = lax.all_gather(table, "ex", axis=0, tiled=True)
    expert = lax.axis_index("ex")
    here = jnp.arange(everyone.shape[1], dtype=jnp.int32)[None, :] == expert
    weight = jnp.sum(jnp.where(here, everyone, 0.0), axis=1, keepdims=True)
    tenant = everyone[:, -1:].astype(jnp.int32)
    mapped = jnp.dot(
        normed, gate_up[0].reshape(width, 2 * hidden_here), preferred_element_type=jnp.float32
    )
    low_rank = jnp.dot(normed, adapter_in[0], preferred_element_type=jnp.float32)
    keep = (jnp.arange(rank_cols, dtype=jnp.int32) // RANK)[None, :] == tenant
    low_rank = jnp.where(keep, low_rank, 0.0).astype(jnp.bfloat16)
    mapped = mapped + jnp.dot(
        low_rank,
        adapter_out[0].reshape(rank_cols, 2 * hidden_here),
        preferred_element_type=jnp.float32,
    )
    gate_part = mapped[:, :hidden_here]
    up_part = mapped[:, hidden_here:]
    activated = (
        gate_part * jax.nn.sigmoid(1.702 * gate_part) * (up_part + 1.0) * weight
    ).astype(jnp.bfloat16)
    terms = jnp.dot(activated, down_proj[0], preferred_element_type=jnp.float32).astype(
        jnp.bfloat16
    )
    return scatter_terms(terms)


def gather_tokens(residual_out):
    tok_rows, columns = residual_out.shape
    sources, quarters = lax.axis_size("ex"), lax.axis_size("tp")
    blocks = lax.all_gather(residual_out, ("ex", "tp"), axis=0, tiled=False)
    blocks = blocks.reshape(sources, quarters, tok_rows, columns).transpose(0, 2, 1, 3)
    return blocks.reshape(sources * tok_rows, quarters * columns)


def scatter_terms(terms):
    mine = lax.psum_scatter(terms, "tp", scatter_dimension=1, tiled=True)
    return lax.psum_scatter(mine, "ex", scatter_dimension=0, tiled=True)


def routed_experts(
    residual_out, norm_gain, routes, route_scores, tenants,
    gate_up, adapter_in, adapter_out, down_proj, columns,
):
    tok_rows = residual_out.shape[0]
    width = gate_up.shape[1]
    whole_rows = lax.all_gather(residual_out, "tp", axis=1, tiled=True).astype(jnp.float32)
    inverse = lax.rsqrt(jnp.mean(whole_rows * whole_rows, axis=-1, keepdims=True) + 1e-05)
    normed = (whole_rows * inverse * norm_gain).astype(jnp.bfloat16)
    sources = lax.axis_size("ex")
    local_count = gate_up.shape[0]
    experts_all = local_count * sources
    capacity = 5 * tok_rows * TOP // (3 * experts_all)
    pair_count = tok_rows * TOP
    route_flat = routes.reshape(pair_count)
    one_hot = (route_flat[:, None] == jnp.arange(experts_all, dtype=jnp.int32)[None, :]).astype(
        jnp.int32
    )
    earlier = jnp.cumsum(one_hot, axis=0) - one_hot
    slot = jnp.sum(earlier * one_hot, axis=1)
    target = route_flat * capacity + slot
    pair_of = (
        jnp.full((experts_all * capacity,), pair_count, jnp.int32)
        .at[target]
        .set(jnp.arange(pair_count, dtype=jnp.int32))
    )
    token_of = pair_of // TOP
    send_width = normed.shape[1]
    normed_pad = jnp.concatenate([normed, jnp.zeros((1, send_width), jnp.bfloat16)], axis=0)
    tenant_pad = jnp.concatenate([tenants, jnp.zeros((1,), jnp.int32)])
    sent_rows = normed_pad[token_of].reshape(experts_all, capacity, send_width)
    sent_tenants = tenant_pad[token_of].reshape(experts_all, capacity)
    received, got_tenants = (
        lax.all_to_all(sent_rows, "ex", split_axis=0, concat_axis=0, tiled=True),
        lax.all_to_all(sent_tenants, "ex", split_axis=0, concat_axis=0, tiled=True),
    )
    hidden_here = gate_up.shape[3]
    rank_cols = adapter_in.shape[2]
    arrived = received.reshape(sources, local_count, capacity, width)
    arrived_tenants = got_tenants.reshape(sources, local_count, capacity)
    slot_rows = arrived[:, 0].reshape(sources * capacity, width)
    slot_tenant = arrived_tenants[:, 0].reshape(sources * capacity)
    mapped = jnp.dot(
        slot_rows, gate_up[0].reshape(width, 2 * hidden_here), preferred_element_type=jnp.float32
    )
    low_rank = jnp.dot(slot_rows, adapter_in[0], preferred_element_type=jnp.float32)
    keep = (jnp.arange(rank_cols, dtype=jnp.int32) // RANK)[None, :] == slot_tenant[:, None]
    low_rank = jnp.where(keep, low_rank, 0.0).astype(jnp.bfloat16)
    mapped = mapped + jnp.dot(
        low_rank,
        adapter_out[0].reshape(rank_cols, 2 * hidden_here),
        preferred_element_type=jnp.float32,
    )
    gate_part = mapped[:, :hidden_here]
    up_part = mapped[:, hidden_here:]
    activated = (gate_part * jax.nn.sigmoid(1.702 * gate_part) * (up_part + 1.0)).astype(
        jnp.bfloat16
    )
    quarter = jnp.dot(activated, down_proj[0], preferred_element_type=jnp.float32).astype(
        jnp.bfloat16
    )
    outputs = quarter.reshape(sources, 1, capacity, width)
    quarters = outputs.reshape(sources * local_count, capacity, width)
    score_float = route_scores.astype(jnp.float32)
    route_weight = (score_float / jnp.sum(score_float, axis=1, keepdims=True)).reshape(pair_count)
    shares = lax.psum_scatter(
        quarters.astype(jnp.float32).astype(jnp.bfloat16), "tp", scatter_dimension=2, tiled=True
    ).astype(jnp.float32)
    returned = lax.all_to_all(
        shares.astype(jnp.bfloat16), "ex", split_axis=0, concat_axis=0, tiled=True
    ).astype(shares.dtype)
    picked = returned.reshape(experts_all * capacity, columns)[target]
    expert_mix = jnp.sum((picked * route_weight[:, None]).reshape(tok_rows, TOP, columns), axis=1)
    return expert_mix.astype(jnp.bfloat16)


def solution(mesh):
    in_specs = (
        P("ex", "tp"),
        P("ex", "tp"),
        P("ex", "tp", None),
        P("tp"),
        P("tp", None),
        P(),
        P("ex", None),
        P("ex", None),
        P("ex"),
        P("ex", None, None, "tp"),
        P("ex", None, None),
        P("ex", None, None, "tp"),
        P("ex", "tp", None),
    )
    out_specs = (P("ex", "tp"), P("ex", "tp"))
    return jax.shard_map(shards, mesh=mesh, in_specs=in_specs, out_specs=out_specs, check_vma=False)
```

```python
import functools

import jax
import jax.numpy as jnp
from jax import lax
from jax.experimental import pallas as pl
from jax.experimental.pallas import tpu as pltpu
from jax.sharding import PartitionSpec as P

WINDOW = 128
TOP = 4
RANK = 16


def from_behind(value, axis, steps):
    count = lax.axis_size(axis)
    initial, last = (max(0, -steps), min(count, count - steps))
    return lax.ppermute(value, axis, [(source, source + steps) for source in range(initial, last)])


def shards(
    residual_in,
    queries,
    keys_values,
    sink_logits,
    out_proj,
    norm_gain,
    routes,
    route_scores,
    tenants,
    gate_up,
    adapter_in,
    adapter_out,
    down_proj,
):
    tok_rows = residual_in.shape[0]
    columns = residual_in.shape[1]
    width = out_proj.shape[1]
    heads_here = sink_logits.shape[0]
    kv_here = keys_values.shape[1]
    group_size = heads_here // kv_here
    head_size = keys_values.shape[2] // 2
    rim_rows = WINDOW - 1
    before = from_behind(keys_values[tok_rows - rim_rows :], "ex", 1)
    extended = jnp.concatenate([before, keys_values], axis=0)
    keys_only = extended[:, :, :head_size]
    values_only = extended[:, :, head_size:]
    query_rows = queries.reshape(tok_rows, kv_here, group_size, head_size)
    scores = jnp.einsum(
        "tcgd,jcd->cgtj", query_rows, keys_only, preferred_element_type=jnp.float32
    ) * head_size ** (-0.5)
    start = lax.axis_index("ex") * tok_rows
    query_pos = start + jnp.arange(tok_rows, dtype=jnp.int32)
    key_pos = start - rim_rows + jnp.arange(tok_rows + rim_rows, dtype=jnp.int32)
    distance = query_pos[:, None] - key_pos[None, :]
    allowed = (distance >= 0) & (distance < WINDOW) & (key_pos[None, :] >= 0)
    numerators = jnp.where(allowed, jnp.exp(scores), 0.0)
    totals = jnp.exp(sink_logits.reshape(kv_here, group_size))[:, :, None] + jnp.sum(
        numerators, axis=-1
    )
    weights = (numerators / totals[..., None]).astype(jnp.bfloat16)
    attended = jnp.einsum(
        "cgtj,jcd->tcgd", weights, values_only, preferred_element_type=jnp.float32
    )
    attended = attended.astype(jnp.bfloat16).reshape(tok_rows, heads_here * head_size)
    head_terms = jnp.dot(attended, out_proj, preferred_element_type=jnp.float32)
    head_share = lax.psum_scatter(
        head_terms.astype(jnp.bfloat16), "tp", scatter_dimension=1, tiled=True
    ).astype(jnp.float32)
    residual_out = (residual_in.astype(jnp.float32) + head_share).astype(jnp.bfloat16)
    sources = lax.axis_size("ex")
    experts_all = gate_up.shape[0] * sources
    capacity = 5 * tok_rows * TOP // (3 * experts_all)
    grouped = lax.axis_size("tp") == 4 and sources % 2 == 0
    if grouped and gate_up.shape[0] == 1 and 2 * capacity >= tok_rows and experts_all <= 256:
        mixed = dense_experts(
            residual_out, routes, route_scores, tenants,
            norm_gain, gate_up, adapter_in, adapter_out, down_proj,
        )
        return (residual_out, mixed)
    return (
        residual_out,
        routed_experts(
            residual_out, norm_gain, routes, route_scores, tenants,
            gate_up, adapter_in, adapter_out, down_proj, columns,
        ),
    )


MESH = pl.DeviceIdType.MESH


def place():
    ex, tp = lax.axis_index("ex"), lax.axis_index("tp")
    return ex // 2, ex % 2, tp // 2, tp % 2


def device(z, y, x, c):
    return (z * 2 + y, x * 2 + c)


def meet(peers):
    barrier = pltpu.get_barrier_semaphore()
    for peer in peers:
        pl.semaphore_signal(barrier, inc=1, device_id=peer, device_id_type=MESH)
    pl.semaphore_wait(barrier, len(peers))


def gather_kernel(
    deep, mine, out, own_sem, z_send, z_recv, x_send, x_recv, y_send, y_recv,
    dx_send, dx_recv, dy_send, dy_recv, c_send, c_recv,
):
    z, y, x, c = place()
    half = mine.shape[0] // 2
    first, second = pl.ds(0, half), pl.ds(half, half)
    at_x, at_y, at_c = device(z, y, 1 - x, c), device(z, 1 - y, x, c), device(z, y, x, 1 - c)
    meet(
        [device(lax.rem(z + k, deep), y, x, c) for k in range(1, deep)] + [at_x, at_y, at_c]
    )

    def send(src, dst, sems, number, to):
        copy = pltpu.make_async_remote_copy(
            src_ref=src, dst_ref=dst, send_sem=sems[0].at[number], recv_sem=sems[1].at[number],
            device_id=to, device_id_type=MESH,
        )
        copy.start()
        return copy

    def whole(k, yy, xx, cc):
        return out.at[lax.rem(z - k + deep, deep), yy, xx, cc]

    own = pltpu.make_async_copy(mine, whole(0, y, x, c), own_sem)
    own.start()
    z_sems, x_sems, y_sems = (z_send, z_recv), (x_send, x_recv), (y_send, y_recv)
    dx_sems, dy_sems, c_sems = (dx_send, dx_recv), (dy_send, dy_recv), (c_send, c_recv)
    sent = []
    down = [None]
    for k in range(1, deep):
        copy = send(mine, whole(0, y, x, c), z_sems, k, device(lax.rem(z + k, deep), y, x, c))
        down.append(copy)
        sent.append(copy)
    to_x, to_y, to_c = [], [], []
    for k in range(deep):
        slot = whole(k, y, x, c)
        if k:
            down[k].wait_recv()
        src = slot if k else mine
        to_x.append(send(src, slot, x_sems, k, at_x))
        to_y.append(send(src, slot, y_sems, k, at_y))
        to_c.append(send(src, slot, c_sems, k, at_c))
    cross_x, cross_y = [], []
    for k in range(deep):
        slot = whole(k, 1 - y, x, c)
        to_y[k].wait_recv()
        cross_x.append(send(slot.at[first], slot.at[first], dx_sems, k, at_x))
        to_c.append(send(slot, slot, c_sems, deep + 2 * k, at_c))
        slot = whole(k, y, 1 - x, c)
        to_x[k].wait_recv()
        cross_y.append(send(slot.at[second], slot.at[second], dy_sems, k, at_y))
        to_c.append(send(slot, slot, c_sems, deep + 2 * k + 1, at_c))
    for k in range(deep):
        slot = whole(k, 1 - y, 1 - x, c)
        cross_x[k].wait_recv()
        to_c.append(send(slot.at[first], slot.at[first], c_sems, 3 * deep + 2 * k, at_c))
        cross_y[k].wait_recv()
        to_c.append(send(slot.at[second], slot.at[second], c_sems, 3 * deep + 2 * k + 1, at_c))
    own.wait()
    for copy in to_c:
        copy.wait_recv()
    for copy in sent + to_x + to_y + cross_x + cross_y + to_c:
        copy.wait_send()


def gather_rows(block):
    deep = lax.axis_size("ex") // 2
    dma = pltpu.SemaphoreType.DMA
    return pl.pallas_call(
        functools.partial(gather_kernel, deep),
        out_shape=jax.ShapeDtypeStruct((deep, 2, 2, 2) + block.shape, block.dtype),
        in_specs=[pl.BlockSpec(memory_space=pltpu.VMEM)],
        out_specs=pl.BlockSpec(memory_space=pl.ANY),
        scratch_shapes=[dma] + [dma((deep,))] * 10 + [dma((5 * deep,))] * 2,
        compiler_params=pltpu.CompilerParams(collective_id=0, has_side_effects=True),
    )(block)


def scatter_kernel(
    deep, terms, out, part, core_in, dx_in, dy_in, x_in, y_in, z_in, c_send, c_recv,
    dx_send, dx_recv, dy_send, dy_recv, x_send, x_recv, y_send, y_recv, z_send, z_recv,
):
    z, y, x, c = place()
    half = out.shape[0] // 2
    first, second = pl.ds(0, half), pl.ds(half, half)
    at_x, at_y, at_c = device(z, y, 1 - x, c), device(z, 1 - y, x, c), device(z, y, x, 1 - c)
    meet(
        [device(lax.rem(z + k, deep), y, x, c) for k in range(1, deep)] + [at_x, at_y, at_c]
    )

    def send(src, dst, sems, number, to):
        copy = pltpu.make_async_remote_copy(
            src_ref=src, dst_ref=dst, send_sem=sems[0].at[number], recv_sem=sems[1].at[number],
            device_id=to, device_id_type=MESH,
        )
        copy.start()
        return copy

    def wide(value):
        return value.astype(jnp.float32)

    z_sems, x_sems, y_sems = (z_send, z_recv), (x_send, x_recv), (y_send, y_recv)
    dx_sems, dy_sems, c_sems = (dx_send, dx_recv), (dy_send, dy_recv), (c_send, c_recv)
    corners = ((1 - y, 1 - x), (1 - y, x), (y, 1 - x), (y, x))

    def far(k):
        return lax.rem(z + deep - 1 - k, deep)

    on_chip = []
    for group, (yy, xx) in enumerate(corners):
        for k in range(deep):
            number = group * deep + k
            on_chip.append(
                send(terms.at[far(k), yy, xx, 1 - c], core_in.at[number], c_sems, number, at_c)
            )

    def add_core(group, k):
        yy, xx = corners[group]
        number = group * deep + k
        on_chip[number].wait_recv()
        part[number] = (
            wide(terms[far(k), yy, xx, c]) + wide(core_in[number])
        ).astype(part.dtype)

    sent = list(on_chip)
    cross_x, cross_y, to_x, to_y, to_z = [], [], [], [], []
    for k in range(deep):
        add_core(0, k)
        cross_x.append(send(part.at[k, first], dx_in.at[k], dx_sems, k, at_x))
        cross_y.append(send(part.at[k, second], dy_in.at[k], dy_sems, k, at_y))
    for k in range(deep):
        add_core(1, k)
        add_core(2, k)
        cross_x[k].wait_recv()
        near = deep + k
        part[near, first] = (wide(part[near, first]) + wide(dx_in[k])).astype(part.dtype)
        to_y.append(send(part.at[near], y_in.at[k], y_sems, k, at_y))
        cross_y[k].wait_recv()
        near = 2 * deep + k
        part[near, second] = (wide(part[near, second]) + wide(dy_in[k])).astype(part.dtype)
        to_x.append(send(part.at[near], x_in.at[k], x_sems, k, at_x))
    for k in range(deep):
        add_core(3, k)
        near = 3 * deep + k
        to_x[k].wait_recv()
        to_y[k].wait_recv()
        part[near] = (wide(part[near]) + wide(x_in[k]) + wide(y_in[k])).astype(part.dtype)
        if k < deep - 1:
            to_z.append(
                send(part.at[near], z_in.at[k], z_sems, k, device(far(k), y, x, c))
            )
    total = wide(part[4 * deep - 1])
    for k in range(deep - 1):
        to_z[k].wait_recv()
        total = total + wide(z_in[k])
    out[...] = total.astype(out.dtype)
    for copy in sent + cross_x + cross_y + to_x + to_y + to_z:
        copy.wait_send()


def scatter_terms(terms):
    deep = lax.axis_size("ex") // 2
    rows, columns = terms.shape[-2:]
    dma = pltpu.SemaphoreType.DMA

    def slots(count, size):
        return pltpu.VMEM((count, size, columns), terms.dtype)

    return pl.pallas_call(
        functools.partial(scatter_kernel, deep),
        out_shape=jax.ShapeDtypeStruct((rows, columns), terms.dtype),
        in_specs=[pl.BlockSpec(memory_space=pltpu.VMEM)],
        out_specs=pl.BlockSpec(memory_space=pltpu.VMEM),
        scratch_shapes=[
            slots(4 * deep, rows), slots(4 * deep, rows), slots(deep, rows // 2),
            slots(deep, rows // 2), slots(deep, rows), slots(deep, rows), slots(deep, rows),
        ]
        + [dma((4 * deep,))] * 2
        + [dma((deep,))] * 10,
        compiler_params=pltpu.CompilerParams(
            collective_id=1, has_side_effects=True, vmem_limit_bytes=60 * 1024 * 1024
        ),
    )(terms.reshape((deep, 2, 2, 2) + terms.shape[-2:]))


def expert_kernel(tokens, gain, weight_gu, weight_in, weight_out, weight_down, terms):
    expert = lax.axis_index("ex")
    held, quarters, tok_rows, padded = tokens.shape
    columns = gain.shape[2]
    rows = held * tok_rows
    hidden = weight_down.shape[1]
    rank_cols = weight_in.shape[2]

    def quarter(q):
        return tokens[:, q].reshape(rows, padded)

    meta = quarter(0)[:, columns : columns + 2 * TOP + 1].astype(jnp.float32)
    routes, scores, tenant = meta[:, :TOP], meta[:, TOP : 2 * TOP], meta[:, 2 * TOP :]
    chosen = jnp.where(routes == expert.astype(jnp.float32), scores, 0.0)
    weight = jnp.sum(chosen, axis=1, keepdims=True) / jnp.sum(scores, axis=1, keepdims=True)
    squares = jnp.zeros((rows, 1), jnp.float32)
    for q in range(quarters):
        wide = quarter(q)[:, :columns].astype(jnp.float32)
        squares += jnp.sum(wide * wide, axis=1, keepdims=True)
    inverse = lax.rsqrt(squares / (quarters * columns) + 1e-05)
    mapped = jnp.zeros((rows, 2 * hidden), jnp.float32)
    low_rank = jnp.zeros((rows, rank_cols), jnp.float32)
    for q in range(quarters):
        wide = quarter(q)[:, :columns].astype(jnp.float32)
        normed = (wide * inverse * gain[q]).astype(jnp.bfloat16)
        mapped += jnp.dot(normed, weight_gu[q], preferred_element_type=jnp.float32)
        low_rank += jnp.dot(normed, weight_in[q], preferred_element_type=jnp.float32)
    owner = lax.broadcasted_iota(jnp.int32, (rows, rank_cols), 1) // RANK
    low_rank = jnp.where(owner == tenant.astype(jnp.int32), low_rank, 0.0).astype(jnp.bfloat16)
    mapped += jnp.dot(low_rank, weight_out[...], preferred_element_type=jnp.float32)
    gate_part, up_part = mapped[:, :hidden], mapped[:, hidden:]
    activated = gate_part * jax.nn.sigmoid(1.702 * gate_part) * (up_part + 1.0)
    activated = (activated * weight).astype(jnp.bfloat16)
    for q in range(quarters):
        term = jnp.dot(activated, weight_down[q], preferred_element_type=jnp.float32)
        terms[:, q] = term.astype(jnp.bfloat16).reshape(held, tok_rows, columns)


def dense_experts(
    residual_out, routes, route_scores, tenants,
    norm_gain, gate_up, adapter_in, adapter_out, down_proj,
):
    tok_rows, columns = residual_out.shape
    sources, quarters = lax.axis_size("ex"), lax.axis_size("tp")
    hidden = gate_up.shape[3]
    rank_cols = adapter_in.shape[2]
    meta = jnp.concatenate([routes, route_scores, tenants[:, None]], axis=1).astype(jnp.bfloat16)
    padded = -(-(columns + meta.shape[1]) // 128) * 128
    fill = jnp.zeros((tok_rows, padded - columns - meta.shape[1]), jnp.bfloat16)
    block = jnp.concatenate([residual_out, meta, fill], axis=1)
    tokens = gather_rows(block).reshape(sources, quarters, tok_rows, padded)
    step = 2
    fixed = lambda *shape: pl.BlockSpec(shape, lambda i: (0,) * len(shape))
    terms = pl.pallas_call(
        expert_kernel,
        grid=(sources // step,),
        out_shape=jax.ShapeDtypeStruct((sources, quarters, tok_rows, columns), jnp.bfloat16),
        in_specs=[
            pl.BlockSpec((step, quarters, tok_rows, padded), lambda i: (i, 0, 0, 0)),
            fixed(quarters, 1, columns),
            fixed(quarters, columns, 2 * hidden),
            fixed(quarters, columns, rank_cols),
            fixed(rank_cols, 2 * hidden),
            fixed(quarters, hidden, columns),
        ],
        out_specs=pl.BlockSpec((step, quarters, tok_rows, columns), lambda i: (i, 0, 0, 0)),
        compiler_params=pltpu.CompilerParams(vmem_limit_bytes=60 * 1024 * 1024),
    )(
        tokens,
        norm_gain.reshape(quarters, 1, columns),
        gate_up[0].reshape(quarters, columns, 2 * hidden),
        adapter_in[0].reshape(quarters, columns, rank_cols),
        adapter_out[0].reshape(rank_cols, 2 * hidden),
        down_proj[0].reshape(hidden, quarters, columns).transpose(1, 0, 2),
    )
    return scatter_terms(terms)


def routed_experts(
    residual_out, norm_gain, routes, route_scores, tenants,
    gate_up, adapter_in, adapter_out, down_proj, columns,
):
    tok_rows = residual_out.shape[0]
    width = gate_up.shape[1]
    whole_rows = lax.all_gather(residual_out, "tp", axis=1, tiled=True).astype(jnp.float32)
    inverse = lax.rsqrt(jnp.mean(whole_rows * whole_rows, axis=-1, keepdims=True) + 1e-05)
    normed = (whole_rows * inverse * norm_gain).astype(jnp.bfloat16)
    sources = lax.axis_size("ex")
    local_count = gate_up.shape[0]
    experts_all = local_count * sources
    capacity = 5 * tok_rows * TOP // (3 * experts_all)
    pair_count = tok_rows * TOP
    route_flat = routes.reshape(pair_count)
    one_hot = (route_flat[:, None] == jnp.arange(experts_all, dtype=jnp.int32)[None, :]).astype(
        jnp.int32
    )
    earlier = jnp.cumsum(one_hot, axis=0) - one_hot
    slot = jnp.sum(earlier * one_hot, axis=1)
    target = route_flat * capacity + slot
    pair_of = (
        jnp.full((experts_all * capacity,), pair_count, jnp.int32)
        .at[target]
        .set(jnp.arange(pair_count, dtype=jnp.int32))
    )
    token_of = pair_of // TOP
    send_width = normed.shape[1]
    normed_pad = jnp.concatenate([normed, jnp.zeros((1, send_width), jnp.bfloat16)], axis=0)
    tenant_pad = jnp.concatenate([tenants, jnp.zeros((1,), jnp.int32)])
    sent_rows = normed_pad[token_of].reshape(experts_all, capacity, send_width)
    sent_tenants = tenant_pad[token_of].reshape(experts_all, capacity)
    received, got_tenants = (
        lax.all_to_all(sent_rows, "ex", split_axis=0, concat_axis=0, tiled=True),
        lax.all_to_all(sent_tenants, "ex", split_axis=0, concat_axis=0, tiled=True),
    )
    hidden_here = gate_up.shape[3]
    rank_cols = adapter_in.shape[2]
    arrived = received.reshape(sources, local_count, capacity, width)
    arrived_tenants = got_tenants.reshape(sources, local_count, capacity)
    slot_rows = arrived[:, 0].reshape(sources * capacity, width)
    slot_tenant = arrived_tenants[:, 0].reshape(sources * capacity)
    mapped = jnp.dot(
        slot_rows, gate_up[0].reshape(width, 2 * hidden_here), preferred_element_type=jnp.float32
    )
    low_rank = jnp.dot(slot_rows, adapter_in[0], preferred_element_type=jnp.float32)
    keep = (jnp.arange(rank_cols, dtype=jnp.int32) // RANK)[None, :] == slot_tenant[:, None]
    low_rank = jnp.where(keep, low_rank, 0.0).astype(jnp.bfloat16)
    mapped = mapped + jnp.dot(
        low_rank,
        adapter_out[0].reshape(rank_cols, 2 * hidden_here),
        preferred_element_type=jnp.float32,
    )
    gate_part = mapped[:, :hidden_here]
    up_part = mapped[:, hidden_here:]
    activated = (gate_part * jax.nn.sigmoid(1.702 * gate_part) * (up_part + 1.0)).astype(
        jnp.bfloat16
    )
    quarter = jnp.dot(activated, down_proj[0], preferred_element_type=jnp.float32).astype(
        jnp.bfloat16
    )
    outputs = quarter.reshape(sources, 1, capacity, width)
    quarters = outputs.reshape(sources * local_count, capacity, width)
    score_float = route_scores.astype(jnp.float32)
    route_weight = (score_float / jnp.sum(score_float, axis=1, keepdims=True)).reshape(pair_count)
    shares = lax.psum_scatter(
        quarters.astype(jnp.float32).astype(jnp.bfloat16), "tp", scatter_dimension=2, tiled=True
    ).astype(jnp.float32)
    returned = lax.all_to_all(
        shares.astype(jnp.bfloat16), "ex", split_axis=0, concat_axis=0, tiled=True
    ).astype(shares.dtype)
    picked = returned.reshape(experts_all * capacity, columns)[target]
    expert_mix = jnp.sum((picked * route_weight[:, None]).reshape(tok_rows, TOP, columns), axis=1)
    return expert_mix.astype(jnp.bfloat16)


def solution(mesh):
    in_specs = (
        P("ex", "tp"),
        P("ex", "tp"),
        P("ex", "tp", None),
        P("tp"),
        P("tp", None),
        P(),
        P("ex", None),
        P("ex", None),
        P("ex"),
        P("ex", None, None, "tp"),
        P("ex", None, None),
        P("ex", None, None, "tp"),
        P("ex", "tp", None),
    )
    out_specs = (P("ex", "tp"), P("ex", "tp"))
    return jax.shard_map(shards, mesh=mesh, in_specs=in_specs, out_specs=out_specs, check_vma=False)
```

```python
import functools

import jax
import jax.numpy as jnp
from jax import lax
from jax.experimental import pallas as pl
from jax.experimental.pallas import tpu as pltpu
from jax.sharding import PartitionSpec as P

WINDOW = 128
TOP = 4
RANK = 16


def from_behind(value, axis, steps):
    count = lax.axis_size(axis)
    initial, last = (max(0, -steps), min(count, count - steps))
    return lax.ppermute(value, axis, [(source, source + steps) for source in range(initial, last)])


def shards(
    residual_in,
    queries,
    keys_values,
    sink_logits,
    out_proj,
    norm_gain,
    routes,
    route_scores,
    tenants,
    gate_up,
    adapter_in,
    adapter_out,
    down_proj,
):
    tok_rows = residual_in.shape[0]
    columns = residual_in.shape[1]
    width = out_proj.shape[1]
    heads_here = sink_logits.shape[0]
    kv_here = keys_values.shape[1]
    group_size = heads_here // kv_here
    head_size = keys_values.shape[2] // 2
    rim_rows = WINDOW - 1
    before = from_behind(keys_values[tok_rows - rim_rows :], "ex", 1)
    extended = jnp.concatenate([before, keys_values], axis=0)
    keys_only = extended[:, :, :head_size]
    values_only = extended[:, :, head_size:]
    query_rows = queries.reshape(tok_rows, kv_here, group_size, head_size)
    scores = jnp.einsum(
        "tcgd,jcd->cgtj", query_rows, keys_only, preferred_element_type=jnp.float32
    ) * head_size ** (-0.5)
    start = lax.axis_index("ex") * tok_rows
    query_pos = start + jnp.arange(tok_rows, dtype=jnp.int32)
    key_pos = start - rim_rows + jnp.arange(tok_rows + rim_rows, dtype=jnp.int32)
    distance = query_pos[:, None] - key_pos[None, :]
    allowed = (distance >= 0) & (distance < WINDOW) & (key_pos[None, :] >= 0)
    numerators = jnp.where(allowed, jnp.exp(scores), 0.0)
    totals = jnp.exp(sink_logits.reshape(kv_here, group_size))[:, :, None] + jnp.sum(
        numerators, axis=-1
    )
    weights = (numerators / totals[..., None]).astype(jnp.bfloat16)
    attended = jnp.einsum(
        "cgtj,jcd->tcgd", weights, values_only, preferred_element_type=jnp.float32
    )
    attended = attended.astype(jnp.bfloat16).reshape(tok_rows, heads_here * head_size)
    head_terms = jnp.dot(attended, out_proj, preferred_element_type=jnp.float32)
    sources = lax.axis_size("ex")
    experts_all = gate_up.shape[0] * sources
    capacity = 5 * tok_rows * TOP // (3 * experts_all)
    grouped = lax.axis_size("tp") == 4 and sources % 2 == 0
    if grouped and gate_up.shape[0] == 1 and 2 * capacity >= tok_rows and experts_all <= 256:
        return dense_experts(
            head_terms, residual_in, routes, route_scores, tenants,
            norm_gain, gate_up, adapter_in, adapter_out, down_proj,
        )
    head_share = lax.psum_scatter(
        head_terms.astype(jnp.bfloat16), "tp", scatter_dimension=1, tiled=True
    ).astype(jnp.float32)
    residual_out = (residual_in.astype(jnp.float32) + head_share).astype(jnp.bfloat16)
    return (
        residual_out,
        routed_experts(
            residual_out, norm_gain, routes, route_scores, tenants,
            gate_up, adapter_in, adapter_out, down_proj, columns,
        ),
    )


MESH = pl.DeviceIdType.MESH


def place():
    ex, tp = lax.axis_index("ex"), lax.axis_index("tp")
    return ex // 2, ex % 2, tp // 2, tp % 2


def device(z, y, x, c):
    return (z * 2 + y, x * 2 + c)


def meet(peers):
    barrier = pltpu.get_barrier_semaphore()
    for peer in peers:
        pl.semaphore_signal(barrier, inc=1, device_id=peer, device_id_type=MESH)
    pl.semaphore_wait(barrier, len(peers))


def gather_kernel(
    deep, heads, base, out, block, mine, core_in, part, x_in, own_sem, h_send, h_recv, z_send, z_recv, x_send, x_recv, y_send, y_recv,
    dx_send, dx_recv, dy_send, dy_recv, c_send, c_recv,
):
    z, y, x, c = place()
    half = mine.shape[0] // 2
    first, second = pl.ds(0, half), pl.ds(half, half)
    at_x, at_y, at_c = device(z, y, 1 - x, c), device(z, 1 - y, x, c), device(z, y, x, 1 - c)
    meet(
        [device(lax.rem(z + k, deep), y, x, c) for k in range(1, deep)] + [at_x, at_y, at_c]
    )

    def send(src, dst, sems, number, to):
        copy = pltpu.make_async_remote_copy(
            src_ref=src, dst_ref=dst, send_sem=sems[0].at[number], recv_sem=sems[1].at[number],
            device_id=to, device_id_type=MESH,
        )
        copy.start()
        return copy

    def whole(k, yy, xx, cc):
        return out.at[lax.rem(z - k + deep, deep), yy, xx, cc]

    h_sems = (h_send, h_recv)
    across = send(heads.at[1 - x, 1 - c], core_in.at[0], h_sems, 0, at_c)
    here = send(heads.at[x, 1 - c], core_in.at[1], h_sems, 1, at_c)
    across.wait_recv()
    part[...] = (
        heads[1 - x, c].astype(jnp.float32) + core_in[0].astype(jnp.float32)
    ).astype(part.dtype)
    over = send(part, x_in, h_sems, 2, at_x)
    here.wait_recv()
    total = base[...].astype(jnp.float32) + (
        heads[x, c].astype(jnp.float32) + core_in[1].astype(jnp.float32)
    )
    over.wait_recv()
    total = (total + x_in[...].astype(jnp.float32)).astype(mine.dtype)
    mine[...] = total
    block[...] = total
    own = pltpu.make_async_copy(mine, whole(0, y, x, c), own_sem)
    own.start()
    z_sems, x_sems, y_sems = (z_send, z_recv), (x_send, x_recv), (y_send, y_recv)
    dx_sems, dy_sems, c_sems = (dx_send, dx_recv), (dy_send, dy_recv), (c_send, c_recv)
    sent = [across, here, over]
    down = [None]
    for k in range(1, deep):
        copy = send(mine, whole(0, y, x, c), z_sems, k, device(lax.rem(z + k, deep), y, x, c))
        down.append(copy)
        sent.append(copy)
    to_x, to_y, to_c = [], [], []
    for k in range(deep):
        slot = whole(k, y, x, c)
        if k:
            down[k].wait_recv()
        src = slot if k else mine
        to_x.append(send(src, slot, x_sems, k, at_x))
        to_y.append(send(src, slot, y_sems, k, at_y))
        to_c.append(send(src, slot, c_sems, k, at_c))
    cross_x, cross_y = [], []
    for k in range(deep):
        slot = whole(k, 1 - y, x, c)
        to_y[k].wait_recv()
        cross_x.append(send(slot.at[first], slot.at[first], dx_sems, k, at_x))
        to_c.append(send(slot, slot, c_sems, deep + 2 * k, at_c))
        slot = whole(k, y, 1 - x, c)
        to_x[k].wait_recv()
        cross_y.append(send(slot.at[second], slot.at[second], dy_sems, k, at_y))
        to_c.append(send(slot, slot, c_sems, deep + 2 * k + 1, at_c))
    for k in range(deep):
        slot = whole(k, 1 - y, 1 - x, c)
        cross_x[k].wait_recv()
        to_c.append(send(slot.at[first], slot.at[first], c_sems, 3 * deep + 2 * k, at_c))
        cross_y[k].wait_recv()
        to_c.append(send(slot.at[second], slot.at[second], c_sems, 3 * deep + 2 * k + 1, at_c))
    own.wait()
    for copy in to_c:
        copy.wait_recv()
    for copy in sent + to_x + to_y + cross_x + cross_y + to_c:
        copy.wait_send()


def gather_rows(heads, base):
    deep = lax.axis_size("ex") // 2
    dma = pltpu.SemaphoreType.DMA
    tile = pltpu.VMEM(base.shape, base.dtype)
    return pl.pallas_call(
        functools.partial(gather_kernel, deep),
        out_shape=(
            jax.ShapeDtypeStruct((deep, 2, 2, 2) + base.shape, base.dtype),
            jax.ShapeDtypeStruct(base.shape, base.dtype),
        ),
        in_specs=[pl.BlockSpec(memory_space=pltpu.VMEM)] * 2,
        out_specs=(pl.BlockSpec(memory_space=pl.ANY), pl.BlockSpec(memory_space=pltpu.VMEM)),
        scratch_shapes=[tile, pltpu.VMEM((2,) + base.shape, base.dtype), tile, tile]
        + [dma, dma((3,)), dma((3,))]
        + [dma((deep,))] * 10
        + [dma((5 * deep,))] * 2,
        compiler_params=pltpu.CompilerParams(collective_id=0, has_side_effects=True),
    )(heads.reshape((2, 2) + base.shape), base)


def scatter_kernel(
    deep, terms, out, part, core_in, dx_in, dy_in, x_in, y_in, z_in, c_send, c_recv,
    dx_send, dx_recv, dy_send, dy_recv, x_send, x_recv, y_send, y_recv, z_send, z_recv,
):
    z, y, x, c = place()
    half = out.shape[0] // 2
    first, second = pl.ds(0, half), pl.ds(half, half)
    at_x, at_y, at_c = device(z, y, 1 - x, c), device(z, 1 - y, x, c), device(z, y, x, 1 - c)
    meet(
        [device(lax.rem(z + k, deep), y, x, c) for k in range(1, deep)] + [at_x, at_y, at_c]
    )

    def send(src, dst, sems, number, to):
        copy = pltpu.make_async_remote_copy(
            src_ref=src, dst_ref=dst, send_sem=sems[0].at[number], recv_sem=sems[1].at[number],
            device_id=to, device_id_type=MESH,
        )
        copy.start()
        return copy

    def wide(value):
        return value.astype(jnp.float32)

    z_sems, x_sems, y_sems = (z_send, z_recv), (x_send, x_recv), (y_send, y_recv)
    dx_sems, dy_sems, c_sems = (dx_send, dx_recv), (dy_send, dy_recv), (c_send, c_recv)
    corners = ((1 - y, 1 - x), (1 - y, x), (y, 1 - x), (y, x))

    def far(k):
        return lax.rem(z + deep - 1 - k, deep)

    on_chip = []
    for group, (yy, xx) in enumerate(corners):
        for k in range(deep):
            number = group * deep + k
            on_chip.append(
                send(terms.at[far(k), yy, xx, 1 - c], core_in.at[number], c_sems, number, at_c)
            )

    def add_core(group, k):
        yy, xx = corners[group]
        number = group * deep + k
        on_chip[number].wait_recv()
        part[number] = (
            wide(terms[far(k), yy, xx, c]) + wide(core_in[number])
        ).astype(part.dtype)

    sent = list(on_chip)
    cross_x, cross_y, to_x, to_y, to_z = [], [], [], [], []
    for k in range(deep):
        add_core(0, k)
        cross_x.append(send(part.at[k, first], dx_in.at[k], dx_sems, k, at_x))
        cross_y.append(send(part.at[k, second], dy_in.at[k], dy_sems, k, at_y))
    for k in range(deep):
        add_core(1, k)
        add_core(2, k)
        cross_x[k].wait_recv()
        near = deep + k
        part[near, first] = (wide(part[near, first]) + wide(dx_in[k])).astype(part.dtype)
        to_y.append(send(part.at[near], y_in.at[k], y_sems, k, at_y))
        cross_y[k].wait_recv()
        near = 2 * deep + k
        part[near, second] = (wide(part[near, second]) + wide(dy_in[k])).astype(part.dtype)
        to_x.append(send(part.at[near], x_in.at[k], x_sems, k, at_x))
    for k in range(deep):
        add_core(3, k)
        near = 3 * deep + k
        to_x[k].wait_recv()
        to_y[k].wait_recv()
        part[near] = (wide(part[near]) + wide(x_in[k]) + wide(y_in[k])).astype(part.dtype)
        if k < deep - 1:
            to_z.append(
                send(part.at[near], z_in.at[k], z_sems, k, device(far(k), y, x, c))
            )
    total = wide(part[4 * deep - 1])
    for k in range(deep - 1):
        to_z[k].wait_recv()
        total = total + wide(z_in[k])
    out[...] = total.astype(out.dtype)
    for copy in sent + cross_x + cross_y + to_x + to_y + to_z:
        copy.wait_send()


def scatter_terms(terms):
    deep = lax.axis_size("ex") // 2
    rows, columns = terms.shape[-2:]
    dma = pltpu.SemaphoreType.DMA

    def slots(count, size):
        return pltpu.VMEM((count, size, columns), terms.dtype)

    return pl.pallas_call(
        functools.partial(scatter_kernel, deep),
        out_shape=jax.ShapeDtypeStruct((rows, columns), terms.dtype),
        in_specs=[pl.BlockSpec(memory_space=pltpu.VMEM)],
        out_specs=pl.BlockSpec(memory_space=pltpu.VMEM),
        scratch_shapes=[
            slots(4 * deep, rows), slots(4 * deep, rows), slots(deep, rows // 2),
            slots(deep, rows // 2), slots(deep, rows), slots(deep, rows), slots(deep, rows),
        ]
        + [dma((4 * deep,))] * 2
        + [dma((deep,))] * 10,
        compiler_params=pltpu.CompilerParams(
            collective_id=1, has_side_effects=True, vmem_limit_bytes=60 * 1024 * 1024
        ),
    )(terms.reshape((deep, 2, 2, 2) + terms.shape[-2:]))


def expert_kernel(tokens, gain, weight_gu, weight_in, weight_out, weight_down, terms):
    expert = lax.axis_index("ex")
    held, quarters, tok_rows, padded = tokens.shape
    columns = gain.shape[2]
    rows = held * tok_rows
    hidden = weight_down.shape[1]
    rank_cols = weight_in.shape[2]

    def quarter(q):
        return tokens[:, q].reshape(rows, padded)

    meta = quarter(0)[:, columns : columns + 2 * TOP + 1].astype(jnp.float32)
    routes, scores, tenant = meta[:, :TOP], meta[:, TOP : 2 * TOP], meta[:, 2 * TOP :]
    chosen = jnp.where(routes == expert.astype(jnp.float32), scores, 0.0)
    weight = jnp.sum(chosen, axis=1, keepdims=True) / jnp.sum(scores, axis=1, keepdims=True)
    squares = jnp.zeros((rows, 1), jnp.float32)
    for q in range(quarters):
        wide = quarter(q)[:, :columns].astype(jnp.float32)
        squares += jnp.sum(wide * wide, axis=1, keepdims=True)
    inverse = lax.rsqrt(squares / (quarters * columns) + 1e-05)
    mapped = jnp.zeros((rows, 2 * hidden), jnp.float32)
    low_rank = jnp.zeros((rows, rank_cols), jnp.float32)
    for q in range(quarters):
        wide = quarter(q)[:, :columns].astype(jnp.float32)
        normed = (wide * inverse * gain[q]).astype(jnp.bfloat16)
        mapped += jnp.dot(normed, weight_gu[q], preferred_element_type=jnp.float32)
        low_rank += jnp.dot(normed, weight_in[q], preferred_element_type=jnp.float32)
    owner = lax.broadcasted_iota(jnp.int32, (rows, rank_cols), 1) // RANK
    low_rank = jnp.where(owner == tenant.astype(jnp.int32), low_rank, 0.0).astype(jnp.bfloat16)
    mapped += jnp.dot(low_rank, weight_out[...], preferred_element_type=jnp.float32)
    gate_part, up_part = mapped[:, :hidden], mapped[:, hidden:]
    activated = gate_part * jax.nn.sigmoid(1.702 * gate_part) * (up_part + 1.0)
    activated = (activated * weight).astype(jnp.bfloat16)
    for q in range(quarters):
        term = jnp.dot(activated, weight_down[q], preferred_element_type=jnp.float32)
        terms[:, q] = term.astype(jnp.bfloat16).reshape(held, tok_rows, columns)


def dense_experts(
    head_terms, residual_in, routes, route_scores, tenants,
    norm_gain, gate_up, adapter_in, adapter_out, down_proj,
):
    tok_rows, columns = residual_in.shape
    sources, quarters = lax.axis_size("ex"), lax.axis_size("tp")
    hidden = gate_up.shape[3]
    rank_cols = adapter_in.shape[2]
    meta = jnp.concatenate([routes, route_scores, tenants[:, None]], axis=1).astype(jnp.bfloat16)
    padded = -(-(columns + meta.shape[1]) // 128) * 128
    fill = jnp.zeros((tok_rows, padded - columns - meta.shape[1]), jnp.bfloat16)
    base = jnp.concatenate([residual_in, meta, fill], axis=1)
    heads = head_terms.astype(jnp.bfloat16)
    heads = [heads[:, q * columns : (q + 1) * columns] for q in range(quarters)]
    heads = jnp.stack([jnp.pad(part, ((0, 0), (0, padded - columns))) for part in heads])
    tokens, block = gather_rows(heads, base)
    tokens = tokens.reshape(sources, quarters, tok_rows, padded)
    step = 2
    fixed = lambda *shape: pl.BlockSpec(shape, lambda i: (0,) * len(shape))
    terms = pl.pallas_call(
        expert_kernel,
        grid=(sources // step,),
        out_shape=jax.ShapeDtypeStruct((sources, quarters, tok_rows, columns), jnp.bfloat16),
        in_specs=[
            pl.BlockSpec((step, quarters, tok_rows, padded), lambda i: (i, 0, 0, 0)),
            fixed(quarters, 1, columns),
            fixed(quarters, columns, 2 * hidden),
            fixed(quarters, columns, rank_cols),
            fixed(rank_cols, 2 * hidden),
            fixed(quarters, hidden, columns),
        ],
        out_specs=pl.BlockSpec((step, quarters, tok_rows, columns), lambda i: (i, 0, 0, 0)),
        compiler_params=pltpu.CompilerParams(vmem_limit_bytes=60 * 1024 * 1024),
    )(
        tokens,
        norm_gain.reshape(quarters, 1, columns),
        gate_up[0].reshape(quarters, columns, 2 * hidden),
        adapter_in[0].reshape(quarters, columns, rank_cols),
        adapter_out[0].reshape(rank_cols, 2 * hidden),
        down_proj[0].reshape(hidden, quarters, columns).transpose(1, 0, 2),
    )
    return (block[:, :columns], scatter_terms(terms))


def routed_experts(
    residual_out, norm_gain, routes, route_scores, tenants,
    gate_up, adapter_in, adapter_out, down_proj, columns,
):
    tok_rows = residual_out.shape[0]
    width = gate_up.shape[1]
    whole_rows = lax.all_gather(residual_out, "tp", axis=1, tiled=True).astype(jnp.float32)
    inverse = lax.rsqrt(jnp.mean(whole_rows * whole_rows, axis=-1, keepdims=True) + 1e-05)
    normed = (whole_rows * inverse * norm_gain).astype(jnp.bfloat16)
    sources = lax.axis_size("ex")
    local_count = gate_up.shape[0]
    experts_all = local_count * sources
    capacity = 5 * tok_rows * TOP // (3 * experts_all)
    pair_count = tok_rows * TOP
    route_flat = routes.reshape(pair_count)
    one_hot = (route_flat[:, None] == jnp.arange(experts_all, dtype=jnp.int32)[None, :]).astype(
        jnp.int32
    )
    earlier = jnp.cumsum(one_hot, axis=0) - one_hot
    slot = jnp.sum(earlier * one_hot, axis=1)
    target = route_flat * capacity + slot
    pair_of = (
        jnp.full((experts_all * capacity,), pair_count, jnp.int32)
        .at[target]
        .set(jnp.arange(pair_count, dtype=jnp.int32))
    )
    token_of = pair_of // TOP
    send_width = normed.shape[1]
    normed_pad = jnp.concatenate([normed, jnp.zeros((1, send_width), jnp.bfloat16)], axis=0)
    tenant_pad = jnp.concatenate([tenants, jnp.zeros((1,), jnp.int32)])
    sent_rows = normed_pad[token_of].reshape(experts_all, capacity, send_width)
    sent_tenants = tenant_pad[token_of].reshape(experts_all, capacity)
    received, got_tenants = (
        lax.all_to_all(sent_rows, "ex", split_axis=0, concat_axis=0, tiled=True),
        lax.all_to_all(sent_tenants, "ex", split_axis=0, concat_axis=0, tiled=True),
    )
    hidden_here = gate_up.shape[3]
    rank_cols = adapter_in.shape[2]
    arrived = received.reshape(sources, local_count, capacity, width)
    arrived_tenants = got_tenants.reshape(sources, local_count, capacity)
    slot_rows = arrived[:, 0].reshape(sources * capacity, width)
    slot_tenant = arrived_tenants[:, 0].reshape(sources * capacity)
    mapped = jnp.dot(
        slot_rows, gate_up[0].reshape(width, 2 * hidden_here), preferred_element_type=jnp.float32
    )
    low_rank = jnp.dot(slot_rows, adapter_in[0], preferred_element_type=jnp.float32)
    keep = (jnp.arange(rank_cols, dtype=jnp.int32) // RANK)[None, :] == slot_tenant[:, None]
    low_rank = jnp.where(keep, low_rank, 0.0).astype(jnp.bfloat16)
    mapped = mapped + jnp.dot(
        low_rank,
        adapter_out[0].reshape(rank_cols, 2 * hidden_here),
        preferred_element_type=jnp.float32,
    )
    gate_part = mapped[:, :hidden_here]
    up_part = mapped[:, hidden_here:]
    activated = (gate_part * jax.nn.sigmoid(1.702 * gate_part) * (up_part + 1.0)).astype(
        jnp.bfloat16
    )
    quarter = jnp.dot(activated, down_proj[0], preferred_element_type=jnp.float32).astype(
        jnp.bfloat16
    )
    outputs = quarter.reshape(sources, 1, capacity, width)
    quarters = outputs.reshape(sources * local_count, capacity, width)
    score_float = route_scores.astype(jnp.float32)
    route_weight = (score_float / jnp.sum(score_float, axis=1, keepdims=True)).reshape(pair_count)
    shares = lax.psum_scatter(
        quarters.astype(jnp.float32).astype(jnp.bfloat16), "tp", scatter_dimension=2, tiled=True
    ).astype(jnp.float32)
    returned = lax.all_to_all(
        shares.astype(jnp.bfloat16), "ex", split_axis=0, concat_axis=0, tiled=True
    ).astype(shares.dtype)
    picked = returned.reshape(experts_all * capacity, columns)[target]
    expert_mix = jnp.sum((picked * route_weight[:, None]).reshape(tok_rows, TOP, columns), axis=1)
    return expert_mix.astype(jnp.bfloat16)


def solution(mesh):
    in_specs = (
        P("ex", "tp"),
        P("ex", "tp"),
        P("ex", "tp", None),
        P("tp"),
        P("tp", None),
        P(),
        P("ex", None),
        P("ex", None),
        P("ex"),
        P("ex", None, None, "tp"),
        P("ex", None, None),
        P("ex", None, None, "tp"),
        P("ex", "tp", None),
    )
    out_specs = (P("ex", "tp"), P("ex", "tp"))
    return jax.shard_map(shards, mesh=mesh, in_specs=in_specs, out_specs=out_specs, check_vma=False)
```

```python
import functools

import jax
import jax.numpy as jnp
from jax import lax
from jax.experimental import pallas as pl
from jax.experimental.pallas import tpu as pltpu
from jax.sharding import PartitionSpec as P

WINDOW = 128
TOP = 4
RANK = 16


def from_behind(value, axis, steps):
    count = lax.axis_size(axis)
    initial, last = (max(0, -steps), min(count, count - steps))
    return lax.ppermute(value, axis, [(source, source + steps) for source in range(initial, last)])


def shards(
    residual_in,
    queries,
    keys_values,
    sink_logits,
    out_proj,
    norm_gain,
    routes,
    route_scores,
    tenants,
    gate_up,
    adapter_in,
    adapter_out,
    down_proj,
):
    tok_rows = residual_in.shape[0]
    columns = residual_in.shape[1]
    width = out_proj.shape[1]
    heads_here = sink_logits.shape[0]
    kv_here = keys_values.shape[1]
    group_size = heads_here // kv_here
    head_size = keys_values.shape[2] // 2
    rim_rows = WINDOW - 1
    before = from_behind(keys_values[tok_rows - rim_rows :], "ex", 1)
    extended = jnp.concatenate([before, keys_values], axis=0)
    keys_only = extended[:, :, :head_size]
    values_only = extended[:, :, head_size:]
    query_rows = queries.reshape(tok_rows, kv_here, group_size, head_size)
    scores = jnp.einsum(
        "tcgd,jcd->cgtj", query_rows, keys_only, preferred_element_type=jnp.float32
    ) * head_size ** (-0.5)
    start = lax.axis_index("ex") * tok_rows
    query_pos = start + jnp.arange(tok_rows, dtype=jnp.int32)
    key_pos = start - rim_rows + jnp.arange(tok_rows + rim_rows, dtype=jnp.int32)
    distance = query_pos[:, None] - key_pos[None, :]
    allowed = (distance >= 0) & (distance < WINDOW) & (key_pos[None, :] >= 0)
    numerators = jnp.where(allowed, jnp.exp(scores), 0.0)
    totals = jnp.exp(sink_logits.reshape(kv_here, group_size))[:, :, None] + jnp.sum(
        numerators, axis=-1
    )
    weights = (numerators / totals[..., None]).astype(jnp.bfloat16)
    attended = jnp.einsum(
        "cgtj,jcd->tcgd", weights, values_only, preferred_element_type=jnp.float32
    )
    attended = attended.astype(jnp.bfloat16).reshape(tok_rows, heads_here * head_size)
    head_terms = jnp.dot(attended, out_proj, preferred_element_type=jnp.float32)
    sources = lax.axis_size("ex")
    experts_all = gate_up.shape[0] * sources
    capacity = 5 * tok_rows * TOP // (3 * experts_all)
    grouped = lax.axis_size("tp") == 4 and sources % 2 == 0
    if grouped and gate_up.shape[0] == 1 and 2 * capacity >= tok_rows and experts_all <= 256:
        return dense_experts(
            head_terms, residual_in, routes, route_scores, tenants,
            norm_gain, gate_up, adapter_in, adapter_out, down_proj,
        )
    head_share = lax.psum_scatter(
        head_terms.astype(jnp.bfloat16), "tp", scatter_dimension=1, tiled=True
    ).astype(jnp.float32)
    residual_out = (residual_in.astype(jnp.float32) + head_share).astype(jnp.bfloat16)
    return (
        residual_out,
        routed_experts(
            residual_out, norm_gain, routes, route_scores, tenants,
            gate_up, adapter_in, adapter_out, down_proj, columns,
        ),
    )


MESH = pl.DeviceIdType.MESH


def place():
    ex, tp = lax.axis_index("ex"), lax.axis_index("tp")
    return ex // 2, ex % 2, tp // 2, tp % 2


def device(z, y, x, c):
    return (z * 2 + y, x * 2 + c)


def meet(peers):
    barrier = pltpu.get_barrier_semaphore()
    for peer in peers:
        pl.semaphore_signal(barrier, inc=1, device_id=peer, device_id_type=MESH)
    pl.semaphore_wait(barrier, len(peers))


def gather_kernel(
    deep, heads, base, out, block, mine, core_in, part, x_in, own_sem, h_send, h_recv, z_send, z_recv, x_send, x_recv, y_send, y_recv,
    dx_send, dx_recv, dy_send, dy_recv, c_send, c_recv,
):
    z, y, x, c = place()
    half = mine.shape[0] // 2
    first, second = pl.ds(0, half), pl.ds(half, half)
    at_x, at_y, at_c = device(z, y, 1 - x, c), device(z, 1 - y, x, c), device(z, y, x, 1 - c)
    meet(
        [device(lax.rem(z + k, deep), y, x, c) for k in range(1, deep)] + [at_x, at_y, at_c]
    )

    def send(src, dst, sems, number, to):
        copy = pltpu.make_async_remote_copy(
            src_ref=src, dst_ref=dst, send_sem=sems[0].at[number], recv_sem=sems[1].at[number],
            device_id=to, device_id_type=MESH,
        )
        copy.start()
        return copy

    def whole(k, yy, xx, cc):
        return out.at[lax.rem(z - k + deep, deep), yy, xx, cc]

    h_sems = (h_send, h_recv)
    across = send(heads.at[1 - x, 1 - c], core_in.at[0], h_sems, 0, at_c)
    here = send(heads.at[x, 1 - c], core_in.at[1], h_sems, 1, at_c)
    across.wait_recv()
    part[...] = (
        heads[1 - x, c].astype(jnp.float32) + core_in[0].astype(jnp.float32)
    ).astype(part.dtype)
    over = send(part, x_in, h_sems, 2, at_x)
    here.wait_recv()
    total = base[...].astype(jnp.float32) + (
        heads[x, c].astype(jnp.float32) + core_in[1].astype(jnp.float32)
    )
    over.wait_recv()
    total = (total + x_in[...].astype(jnp.float32)).astype(mine.dtype)
    mine[...] = total
    block[...] = total
    own = pltpu.make_async_copy(mine, whole(0, y, x, c), own_sem)
    own.start()
    z_sems, x_sems, y_sems = (z_send, z_recv), (x_send, x_recv), (y_send, y_recv)
    dx_sems, dy_sems, c_sems = (dx_send, dx_recv), (dy_send, dy_recv), (c_send, c_recv)
    sent = [across, here, over]
    down = [None]
    for k in range(1, deep):
        copy = send(mine, whole(0, y, x, c), z_sems, k, device(lax.rem(z + k, deep), y, x, c))
        down.append(copy)
        sent.append(copy)
    to_x, to_y, to_c = [], [], []
    for k in range(deep):
        slot = whole(k, y, x, c)
        if k:
            down[k].wait_recv()
        src = slot if k else mine
        to_x.append(send(src, slot, x_sems, k, at_x))
        to_y.append(send(src, slot, y_sems, k, at_y))
        to_c.append(send(src, slot, c_sems, k, at_c))
    cross_x, cross_y = [], []
    for k in range(deep):
        slot = whole(k, 1 - y, x, c)
        to_y[k].wait_recv()
        cross_x.append(send(slot.at[first], slot.at[first], dx_sems, k, at_x))
        to_c.append(send(slot, slot, c_sems, deep + 2 * k, at_c))
        slot = whole(k, y, 1 - x, c)
        to_x[k].wait_recv()
        cross_y.append(send(slot.at[second], slot.at[second], dy_sems, k, at_y))
        to_c.append(send(slot, slot, c_sems, deep + 2 * k + 1, at_c))
    for k in range(deep):
        slot = whole(k, 1 - y, 1 - x, c)
        cross_x[k].wait_recv()
        to_c.append(send(slot.at[first], slot.at[first], c_sems, 3 * deep + 2 * k, at_c))
        cross_y[k].wait_recv()
        to_c.append(send(slot.at[second], slot.at[second], c_sems, 3 * deep + 2 * k + 1, at_c))
    own.wait()
    for copy in to_c:
        copy.wait_recv()
    for copy in sent + to_x + to_y + cross_x + cross_y + to_c:
        copy.wait_send()


def gather_rows(heads, base):
    deep = lax.axis_size("ex") // 2
    dma = pltpu.SemaphoreType.DMA
    tile = pltpu.VMEM(base.shape, base.dtype)
    return pl.pallas_call(
        functools.partial(gather_kernel, deep),
        out_shape=(
            jax.ShapeDtypeStruct((deep, 2, 2, 2) + base.shape, base.dtype),
            jax.ShapeDtypeStruct(base.shape, base.dtype),
        ),
        in_specs=[pl.BlockSpec(memory_space=pltpu.VMEM)] * 2,
        out_specs=(pl.BlockSpec(memory_space=pl.ANY), pl.BlockSpec(memory_space=pltpu.VMEM)),
        scratch_shapes=[tile, pltpu.VMEM((2,) + base.shape, base.dtype), tile, tile]
        + [dma, dma((3,)), dma((3,))]
        + [dma((deep,))] * 10
        + [dma((5 * deep,))] * 2,
        compiler_params=pltpu.CompilerParams(collective_id=0, has_side_effects=True),
    )(heads.reshape((2, 2) + base.shape), base)


def scatter_kernel(
    deep, terms, out, part, core_in, dx_in, dy_in, x_in, y_in, z_in, c_send, c_recv,
    dx_send, dx_recv, dy_send, dy_recv, x_send, x_recv, y_send, y_recv, z_send, z_recv,
):
    z, y, x, c = place()
    half = out.shape[0] // 2
    first, second = pl.ds(0, half), pl.ds(half, half)
    at_x, at_y, at_c = device(z, y, 1 - x, c), device(z, 1 - y, x, c), device(z, y, x, 1 - c)
    meet(
        [device(lax.rem(z + k, deep), y, x, c) for k in range(1, deep)] + [at_x, at_y, at_c]
    )

    def send(src, dst, sems, number, to):
        copy = pltpu.make_async_remote_copy(
            src_ref=src, dst_ref=dst, send_sem=sems[0].at[number], recv_sem=sems[1].at[number],
            device_id=to, device_id_type=MESH,
        )
        copy.start()
        return copy

    def wide(value):
        return value.astype(jnp.float32)

    z_sems, x_sems, y_sems = (z_send, z_recv), (x_send, x_recv), (y_send, y_recv)
    dx_sems, dy_sems, c_sems = (dx_send, dx_recv), (dy_send, dy_recv), (c_send, c_recv)
    corners = ((1 - y, 1 - x), (1 - y, x), (y, 1 - x), (y, x))

    def far(k):
        return lax.rem(z + deep - 1 - k, deep)

    on_chip = []
    for group, (yy, xx) in enumerate(corners):
        for k in range(deep):
            number = group * deep + k
            on_chip.append(
                send(terms.at[far(k), yy, xx, 1 - c], core_in.at[number], c_sems, number, at_c)
            )

    def add_core(group, k):
        yy, xx = corners[group]
        number = group * deep + k
        on_chip[number].wait_recv()
        part[number] = (
            wide(terms[far(k), yy, xx, c]) + wide(core_in[number])
        ).astype(part.dtype)

    sent = list(on_chip)
    cross_x, cross_y, to_x, to_y, to_z = [], [], [], [], []
    for k in range(deep):
        add_core(0, k)
        cross_x.append(send(part.at[k, first], dx_in.at[k], dx_sems, k, at_x))
        cross_y.append(send(part.at[k, second], dy_in.at[k], dy_sems, k, at_y))
    for k in range(deep):
        add_core(1, k)
        add_core(2, k)
        cross_x[k].wait_recv()
        near = deep + k
        part[near, first] = (wide(part[near, first]) + wide(dx_in[k])).astype(part.dtype)
        to_y.append(send(part.at[near], y_in.at[k], y_sems, k, at_y))
        cross_y[k].wait_recv()
        near = 2 * deep + k
        part[near, second] = (wide(part[near, second]) + wide(dy_in[k])).astype(part.dtype)
        to_x.append(send(part.at[near], x_in.at[k], x_sems, k, at_x))
    for k in range(deep):
        add_core(3, k)
        near = 3 * deep + k
        to_x[k].wait_recv()
        to_y[k].wait_recv()
        part[near] = (wide(part[near]) + wide(x_in[k]) + wide(y_in[k])).astype(part.dtype)
        if k < deep - 1:
            to_z.append(
                send(part.at[near], z_in.at[k], z_sems, k, device(far(k), y, x, c))
            )
    total = wide(part[4 * deep - 1])
    for k in range(deep - 1):
        to_z[k].wait_recv()
        total = total + wide(z_in[k])
    out[...] = total.astype(out.dtype)
    for copy in sent + cross_x + cross_y + to_x + to_y + to_z:
        copy.wait_send()


def scatter_terms(terms):
    deep = lax.axis_size("ex") // 2
    rows, columns = terms.shape[-2:]
    dma = pltpu.SemaphoreType.DMA

    def slots(count, size):
        return pltpu.VMEM((count, size, columns), terms.dtype)

    return pl.pallas_call(
        functools.partial(scatter_kernel, deep),
        out_shape=jax.ShapeDtypeStruct((rows, columns), terms.dtype),
        in_specs=[pl.BlockSpec(memory_space=pltpu.VMEM)],
        out_specs=pl.BlockSpec(memory_space=pltpu.VMEM),
        scratch_shapes=[
            slots(4 * deep, rows), slots(4 * deep, rows), slots(deep, rows // 2),
            slots(deep, rows // 2), slots(deep, rows), slots(deep, rows), slots(deep, rows),
        ]
        + [dma((4 * deep,))] * 2
        + [dma((deep,))] * 10,
        compiler_params=pltpu.CompilerParams(
            collective_id=1, has_side_effects=True, vmem_limit_bytes=60 * 1024 * 1024
        ),
    )(terms.reshape((deep, 2, 2, 2) + terms.shape[-2:]))


def expert_kernel(tokens, gain, weight_gu, weight_in, weight_out, weight_down, terms):
    expert = lax.axis_index("ex")
    held, quarters, tok_rows, padded = tokens.shape
    columns = gain.shape[2]
    rows = held * tok_rows
    hidden = weight_down.shape[2]
    rank_cols = weight_in.shape[2]

    def quarter(q):
        return tokens[:, q].reshape(rows, padded)

    meta = quarter(0)[:, columns : columns + 2 * TOP + 1].astype(jnp.float32)
    routes, scores, tenant = meta[:, :TOP], meta[:, TOP : 2 * TOP], meta[:, 2 * TOP :]
    chosen = jnp.where(routes == expert.astype(jnp.float32), scores, 0.0)
    weight = jnp.sum(chosen, axis=1, keepdims=True) / jnp.sum(scores, axis=1, keepdims=True)
    squares = jnp.zeros((rows, 1), jnp.float32)
    for q in range(quarters):
        wide = quarter(q)[:, :columns].astype(jnp.float32)
        squares += jnp.sum(wide * wide, axis=1, keepdims=True)
    inverse = lax.rsqrt(squares / (quarters * columns) + 1e-05)
    mapped = jnp.zeros((rows, 2 * hidden), jnp.float32)
    low_rank = jnp.zeros((rows, rank_cols), jnp.float32)
    for q in range(quarters):
        wide = quarter(q)[:, :columns].astype(jnp.float32)
        normed = (wide * inverse * gain[q]).astype(jnp.bfloat16)
        mapped += jnp.dot(normed, weight_gu[q], preferred_element_type=jnp.float32)
        low_rank += jnp.dot(normed, weight_in[q], preferred_element_type=jnp.float32)
    owner = lax.broadcasted_iota(jnp.int32, (rows, rank_cols), 1) // RANK
    low_rank = jnp.where(owner == tenant.astype(jnp.int32), low_rank, 0.0).astype(jnp.bfloat16)
    mapped += jnp.dot(low_rank, weight_out[...], preferred_element_type=jnp.float32)
    gate_part, up_part = mapped[:, :hidden], mapped[:, hidden:]
    activated = gate_part * jax.nn.sigmoid(1.702 * gate_part) * (up_part + 1.0)
    activated = (activated * weight).astype(jnp.bfloat16)
    for q in range(quarters):
        term = lax.dot_general(
            activated, weight_down[q], (((1,), (1,)), ((), ())), preferred_element_type=jnp.float32
        )
        terms[:, q] = term.astype(jnp.bfloat16).reshape(held, tok_rows, columns)


def dense_experts(
    head_terms, residual_in, routes, route_scores, tenants,
    norm_gain, gate_up, adapter_in, adapter_out, down_proj,
):
    tok_rows, columns = residual_in.shape
    sources, quarters = lax.axis_size("ex"), lax.axis_size("tp")
    hidden = gate_up.shape[3]
    rank_cols = adapter_in.shape[2]
    meta = jnp.concatenate([routes, route_scores, tenants[:, None]], axis=1).astype(jnp.bfloat16)
    padded = -(-(columns + meta.shape[1]) // 128) * 128
    fill = jnp.zeros((tok_rows, padded - columns - meta.shape[1]), jnp.bfloat16)
    base = jnp.concatenate([residual_in, meta, fill], axis=1)
    heads = head_terms.astype(jnp.bfloat16)
    heads = [heads[:, q * columns : (q + 1) * columns] for q in range(quarters)]
    heads = jnp.stack([jnp.pad(part, ((0, 0), (0, padded - columns))) for part in heads])
    tokens, block = gather_rows(heads, base)
    tokens = tokens.reshape(sources, quarters, tok_rows, padded)
    step = 2
    fixed = lambda *shape: pl.BlockSpec(shape, lambda i: (0,) * len(shape))
    terms = pl.pallas_call(
        expert_kernel,
        grid=(sources // step,),
        out_shape=jax.ShapeDtypeStruct((sources, quarters, tok_rows, columns), jnp.bfloat16),
        in_specs=[
            pl.BlockSpec((step, quarters, tok_rows, padded), lambda i: (i, 0, 0, 0)),
            fixed(quarters, 1, columns),
            fixed(quarters, columns, 2 * hidden),
            fixed(quarters, columns, rank_cols),
            fixed(rank_cols, 2 * hidden),
            fixed(quarters, columns, hidden),
        ],
        out_specs=pl.BlockSpec((step, quarters, tok_rows, columns), lambda i: (i, 0, 0, 0)),
        compiler_params=pltpu.CompilerParams(vmem_limit_bytes=60 * 1024 * 1024),
    )(
        tokens,
        norm_gain.reshape(quarters, 1, columns),
        jnp.concatenate([gate_up[0, :, 0], gate_up[0, :, 1]], axis=1).reshape(
            quarters, columns, 2 * hidden
        ),
        adapter_in[0].reshape(quarters, columns, rank_cols),
        adapter_out[0].reshape(rank_cols, 2 * hidden),
        down_proj[0].T.reshape(quarters, columns, hidden),
    )
    return (block[:, :columns], scatter_terms(terms))


def routed_experts(
    residual_out, norm_gain, routes, route_scores, tenants,
    gate_up, adapter_in, adapter_out, down_proj, columns,
):
    tok_rows = residual_out.shape[0]
    width = gate_up.shape[1]
    whole_rows = lax.all_gather(residual_out, "tp", axis=1, tiled=True).astype(jnp.float32)
    inverse = lax.rsqrt(jnp.mean(whole_rows * whole_rows, axis=-1, keepdims=True) + 1e-05)
    normed = (whole_rows * inverse * norm_gain).astype(jnp.bfloat16)
    sources = lax.axis_size("ex")
    local_count = gate_up.shape[0]
    experts_all = local_count * sources
    capacity = 5 * tok_rows * TOP // (3 * experts_all)
    pair_count = tok_rows * TOP
    route_flat = routes.reshape(pair_count)
    one_hot = (route_flat[:, None] == jnp.arange(experts_all, dtype=jnp.int32)[None, :]).astype(
        jnp.int32
    )
    earlier = jnp.cumsum(one_hot, axis=0) - one_hot
    slot = jnp.sum(earlier * one_hot, axis=1)
    target = route_flat * capacity + slot
    pair_of = (
        jnp.full((experts_all * capacity,), pair_count, jnp.int32)
        .at[target]
        .set(jnp.arange(pair_count, dtype=jnp.int32))
    )
    token_of = pair_of // TOP
    send_width = normed.shape[1]
    normed_pad = jnp.concatenate([normed, jnp.zeros((1, send_width), jnp.bfloat16)], axis=0)
    tenant_pad = jnp.concatenate([tenants, jnp.zeros((1,), jnp.int32)])
    sent_rows = normed_pad[token_of].reshape(experts_all, capacity, send_width)
    sent_tenants = tenant_pad[token_of].reshape(experts_all, capacity)
    received, got_tenants = (
        lax.all_to_all(sent_rows, "ex", split_axis=0, concat_axis=0, tiled=True),
        lax.all_to_all(sent_tenants, "ex", split_axis=0, concat_axis=0, tiled=True),
    )
    hidden_here = gate_up.shape[3]
    rank_cols = adapter_in.shape[2]
    arrived = received.reshape(sources, local_count, capacity, width)
    arrived_tenants = got_tenants.reshape(sources, local_count, capacity)
    slot_rows = arrived[:, 0].reshape(sources * capacity, width)
    slot_tenant = arrived_tenants[:, 0].reshape(sources * capacity)
    mapped = jnp.dot(
        slot_rows, gate_up[0].reshape(width, 2 * hidden_here), preferred_element_type=jnp.float32
    )
    low_rank = jnp.dot(slot_rows, adapter_in[0], preferred_element_type=jnp.float32)
    keep = (jnp.arange(rank_cols, dtype=jnp.int32) // RANK)[None, :] == slot_tenant[:, None]
    low_rank = jnp.where(keep, low_rank, 0.0).astype(jnp.bfloat16)
    mapped = mapped + jnp.dot(
        low_rank,
        adapter_out[0].reshape(rank_cols, 2 * hidden_here),
        preferred_element_type=jnp.float32,
    )
    gate_part = mapped[:, :hidden_here]
    up_part = mapped[:, hidden_here:]
    activated = (gate_part * jax.nn.sigmoid(1.702 * gate_part) * (up_part + 1.0)).astype(
        jnp.bfloat16
    )
    quarter = jnp.dot(activated, down_proj[0], preferred_element_type=jnp.float32).astype(
        jnp.bfloat16
    )
    outputs = quarter.reshape(sources, 1, capacity, width)
    quarters = outputs.reshape(sources * local_count, capacity, width)
    score_float = route_scores.astype(jnp.float32)
    route_weight = (score_float / jnp.sum(score_float, axis=1, keepdims=True)).reshape(pair_count)
    shares = lax.psum_scatter(
        quarters.astype(jnp.float32).astype(jnp.bfloat16), "tp", scatter_dimension=2, tiled=True
    ).astype(jnp.float32)
    returned = lax.all_to_all(
        shares.astype(jnp.bfloat16), "ex", split_axis=0, concat_axis=0, tiled=True
    ).astype(shares.dtype)
    picked = returned.reshape(experts_all * capacity, columns)[target]
    expert_mix = jnp.sum((picked * route_weight[:, None]).reshape(tok_rows, TOP, columns), axis=1)
    return expert_mix.astype(jnp.bfloat16)


def solution(mesh):
    in_specs = (
        P("ex", "tp"),
        P("ex", "tp"),
        P("ex", "tp", None),
        P("tp"),
        P("tp", None),
        P(),
        P("ex", None),
        P("ex", None),
        P("ex"),
        P("ex", None, None, "tp"),
        P("ex", None, None),
        P("ex", None, None, "tp"),
        P("ex", "tp", None),
    )
    out_specs = (P("ex", "tp"), P("ex", "tp"))
    return jax.shard_map(shards, mesh=mesh, in_specs=in_specs, out_specs=out_specs, check_vma=False)
```
